512 devices in a mesh: seq: 64 (over x, y, core), tp: 8 (over z).
Axes of the slice: x: 4, y: 8, z: 8, core: 2. Of those that a mesh axis runs over, the one named last changes fastest.
Arguments:
- queries: bfloat16 [16384, 4096], P('seq', 'tp'), may hold values from -50 to 50
- keys: bfloat16 [16384, 4096], P('seq', 'tp'), may hold values from -4 to 4
- values: bfloat16 [16384, 4096], P('seq', 'tp'), may hold values from -18 to 18
- doc_lengths: int32 [32], replicated, may hold values from 1 to 2048, 16384 in all
- out_weight: bfloat16 [4096, 4096], P('tp', 'seq'), may hold values from -0.25 to 0.25
Outputs:
- projected: bfloat16 [16384, 4096], P('seq', 'tp')
The draws below stay inside these ranges and needn't reach their ends.
Inputs may be any that keep to these rules, and one draw needn't show every extreme that they name: `doc_lengths`: document lengths in order, summing to 16384; the longest is exactly 2048.
All inputs are finite; a program needn't handle non-finite values.
Results may differ from the reference program's by a relative error of at most 0.015.
Values may be sent and summed in bfloat16 or wider, within the bound.
No kernel may reach another device: no remote copies, remote signals or barrier semaphores. Data moves between devices by JAX's collectives and lax.ppermute only.
A program may use at most 64 MiB of HBM per device.

```python
import math
import jax
import jax.numpy as jnp
import numpy as np
from jax import lax

D = 4096
HEADS = 32
HD = 128
TOK_DEV = 256
NDOC = 32
MOST = 2048
TOKENS = 16384
HW = 4096


def draw_pair(key):
    base = jax.random.fold_in(key, 17)
    key_one, key_two = jax.random.split(base, 2)
    shape = (TOKENS, HEADS * HD)
    keys_f = jnp.clip(jax.random.normal(key_one, shape, jnp.float32), -4.0, 4.0)
    queries_f = jnp.clip(jax.random.normal(key_two, shape, jnp.float32), -4.0, 4.0)
    return (queries_f.astype(jnp.bfloat16), keys_f.astype(jnp.bfloat16))


def draw_queries(key, part):
    return draw_pair(key)[0]


def draw_keys(key, part):
    return draw_pair(key)[1]


def spiked(values, rng, source, target, parts, factor):
    owner, partner = [(jnp.arange(values.shape[dim]) // (values.shape[dim] // parts)).reshape([-1 if axis == dim else 1 for axis in range(values.ndim)]) for dim in (source, target)]
    chosen = jax.random.permutation(rng, parts)[partner]
    strong = (owner == chosen) | (owner == (partner + parts // 2) % parts)
    return jnp.where(strong, factor * values, values)


def shard_levels(own_key, shape, cuts, least, high):
    def one(dim, blocks):
        steps = jax.random.uniform(jax.random.fold_in(jax.random.fold_in(own_key, 6), dim), (blocks,), jnp.float32, least / len(cuts), high / len(cuts))
        return jnp.repeat(jnp.exp(steps), shape[dim] // blocks).reshape((-1,) + (1,) * (len(shape) - dim - 1))

    gain = one(*cuts[0])
    for cut in cuts[1:]:
        gain = gain * one(*cut)
    return gain


def length_profile(number_of, total, limit, lean):
    weights = [(1 << 20) // math.isqrt(standing ** lean) + 1 for standing in range(2, number_of + 1)]
    spare, given = total - limit - (number_of - 1), [1] * (number_of - 1)
    while spare > 0:
        candidates = [i for i in range(number_of - 1) if given[i] < limit]
        pool, budget = sum([weights[i] for i in candidates]), spare
        for i in candidates:
            extra = min(limit - given[i], max(1, budget * weights[i] // pool), spare)
            given[i] = given[i] + extra
            spare = spare - extra
    return np.array([limit] + given)


def ragged(stream_key, count, total, reach, skew):
    if count == 2:
        one = jax.random.randint(stream_key, (), max(1, total - reach), min(reach, total - 1) + 1)
        return jnp.stack([one, total - one])
    lengths = jnp.asarray(length_profile(count, total, reach, skew), jnp.int32)
    twos = (count - 1) // 2
    source_of, taker = lengths[1:1 + 2 * twos:2], lengths[2:2 + 2 * twos:2]
    margin = jnp.minimum(source_of - 1, reach - taker)
    moved = jax.random.randint(jax.random.fold_in(stream_key, 1), (twos,), 0, 1 << 20) % (margin + 1)
    lengths = lengths.at[1:1 + 2 * twos:2].set(source_of - moved).at[2:2 + 2 * twos:2].set(taker + moved)
    return lengths[jax.random.permutation(jax.random.fold_in(stream_key, 2), count)]


def noise(stream_key, dims, width, bound, cuts=(), held_as=jnp.bfloat16):
    drawn = jax.random.normal(stream_key, dims, jnp.float32) * width
    if len(cuts) > 0:
        drawn = shard_levels(stream_key, dims, cuts, -0.22, 0.18) * drawn
    return jnp.clip(drawn, min=-bound, max=bound).astype(held_as)


def bell_draw_with(stream_key, dims, deviation, most, cuts, heavy, kind=jnp.bfloat16):
    drawn = deviation * jax.random.normal(stream_key, dims, jnp.float32)
    if cuts:
        drawn = drawn * shard_levels(stream_key, dims, cuts, -0.22, 0.18)
    return jnp.clip(spiked(drawn, jax.random.fold_in(stream_key, 3), *heavy), -most, most).astype(kind)


def setup_inputs(seed: int = 0) -> dict:
    key_of = jax.random.split(jax.random.key(seed), 6)
    queries = draw_queries(jax.random.fold_in(key_of[5], 71), 0)
    keys = draw_keys(jax.random.fold_in(key_of[5], 71), 0)
    values = noise(key_of[2], (TOKENS, HW), 3.0, 18.0, ((0, 64), (1, 8)))
    doc_lengths = ragged(key_of[3], NDOC, TOKENS, MOST, 2).astype(jnp.int32)
    out_weight = bell_draw_with(key_of[4], (HW, D), HW ** -0.5, 0.25, ((0, 8), (1, 64)), (0, 1, 64, 4.0))
    return dict(queries=queries, keys=keys, values=values, doc_lengths=doc_lengths, out_weight=out_weight)


def doc_of(positions, doc_lengths):
    ends = jnp.cumsum(doc_lengths).astype(jnp.int32)
    return jnp.sum((ends[None, :] <= positions[:, None]).astype(jnp.int32), axis=1).astype(jnp.int32)


def reference(queries, keys, values, doc_lengths, out_weight):
    scale = 1.0 / (HD ** 0.5)
    token_ids = doc_of(jnp.arange(TOKENS, dtype=jnp.int32), doc_lengths)
    pad_rows = jnp.zeros((MOST, HEADS * HD), jnp.bfloat16)
    keys_pad = jnp.concatenate([pad_rows, keys, pad_rows], axis=0)
    values_pad = jnp.concatenate([pad_rows, values, pad_rows], axis=0)
    pad_ids = jnp.full((MOST,), -1, jnp.int32)
    ids_pad = jnp.concatenate([pad_ids, token_ids, pad_ids], axis=0)
    span = TOK_DEV + 2 * MOST

    def one_block(block):
        start = (block * TOK_DEV).astype(jnp.int32)
        query_blk = lax.dynamic_slice_in_dim(queries, start, TOK_DEV, 0).astype(jnp.float32).reshape(TOK_DEV, HEADS, HD)
        key_blk = lax.dynamic_slice_in_dim(keys_pad, start, span, 0).astype(jnp.float32).reshape(span, HEADS, HD)
        value_blk = lax.dynamic_slice_in_dim(values_pad, start, span, 0).astype(jnp.float32).reshape(span, HEADS, HD)
        query_ids = lax.dynamic_slice_in_dim(token_ids, start, TOK_DEV, 0)
        key_ids = lax.dynamic_slice_in_dim(ids_pad, start, span, 0)
        same = (query_ids[:, None] == key_ids[None, :])[None]
        scores = jnp.einsum("qhd,khd->hqk", query_blk, key_blk) * scale
        scores = jnp.where(same, scores, -1e30)
        top = jnp.max(scores, axis=2, keepdims=True)
        weights = jnp.where(same, jnp.exp(scores - top), 0.0)
        totals = jnp.sum(weights, axis=2)
        rounded = lax.optimization_barrier(weights.astype(jnp.bfloat16)).astype(jnp.float32)
        mixed = jnp.einsum("hqk,khd->hqd", rounded, value_blk) / totals[:, :, None]
        return jnp.transpose(mixed, (1, 0, 2)).reshape(TOK_DEV, HEADS * HD).astype(jnp.bfloat16)

    attended = lax.map(one_block, jnp.arange(TOKENS // TOK_DEV, dtype=jnp.int32)).reshape(TOKENS, HEADS * HD)
    return jnp.dot(attended, out_weight, preferred_element_type=jnp.float32).astype(jnp.bfloat16)
```

```python
import functools
import math

import jax
import jax.numpy as jnp
from jax import lax
from jax.experimental import pallas as pl
from jax.experimental.pallas import tpu as pltpu
from jax.sharding import PartitionSpec as P


HD = 128
X, Y, Z = 4, 8, 8
HOPS = 4
LOW = -1e30
MASKED = -3e37
C2 = math.log2(math.e) / math.sqrt(HD)


def device(x, y, core):
    return ((x % X) * Y + y % Y) * 2 + core


def pairs_of(step):
    return [
        (device(x, y, core), device(*step(x, y, core)))
        for x in range(X)
        for y in range(Y)
        for core in range(2)
    ]


SWAP = pairs_of(lambda x, y, core: (x, y, 1 - core))
Y_WAYS = pairs_of(lambda x, y, core: (x, y + 1 - 2 * core, core))
X_FAR = {far: pairs_of(lambda x, y, core, far=far: (x + far, y, core)) for far in range(1, X)}
SIDES = [(s, s + 2 - 4 * (s % 2)) for s in range(2 * X * Y) if 0 <= s + 2 - 4 * (s % 2) < 2 * X * Y]
Z_UP = [(z, (z + 1) % Z) for z in range(Z)]
Z_DOWN = [(z, (z - 1) % Z) for z in range(Z)]
TURN = [
    ((8 * a + j) * Z + b, (8 * b + j) * Z + a) for a in range(Z) for b in range(Z) for j in range(8)
]


def attend_kernel(first, blocks, scal, bounds, q_own, q_par, *refs):
    count = len(blocks)
    kvs = refs[:count]
    if first:
        outs = refs[count:]
        for out in outs:
            out[0:512, :] = jnp.zeros((512, 256), jnp.float32)
            row = lax.broadcasted_iota(jnp.int32, (32, 256), 0)
            out[512:544, :] = jnp.where(row % 8 == 0, LOW, 0.0)
    else:
        ins = refs[count : count + 2]
        outs = refs[count + 2 :]
        for given, out in zip(ins, outs, strict=True):
            out[...] = given[...]

    for half, (q_ref, state) in enumerate(zip((q_own, q_par), outs, strict=True)):
        low_first, high_last = scal[16 + 4 * half], scal[19 + 4 * half]

        def tile(kv, start, half=half, q_ref=q_ref, state=state):
            wide = 256
            spot = lax.broadcasted_iota(jnp.int32, (256, wide), 0) + start
            jobs = [(head, part) for part in range(256 // wide) for head in range(4)]

            def score(job):
                head, part = job
                lanes = slice(head * HD, (head + 1) * HD)
                return lax.dot_general(
                    kv[0:256, lanes],
                    q_ref[part * wide : (part + 1) * wide, lanes],
                    (((1,), (1,)), ((), ())),
                    preferred_element_type=jnp.float32,
                )

            keeps = []
            for part in range(256 // wide):
                columns = slice(part * wide, (part + 1) * wide)
                keeps.append(
                    (spot >= bounds[2 * half : 2 * half + 1, columns])
                    & (spot < bounds[2 * half + 1 : 2 * half + 2, columns])
                )
            ahead = {number: score(jobs[number]) for number in range(2)}
            for number, (head, part) in enumerate(jobs):
                columns = slice(part * wide, (part + 1) * wide)
                lanes = slice(head * HD, (head + 1) * HD)
                stats = slice(512 + 8 * head, 520 + 8 * head)
                if number + 2 < len(jobs):
                    ahead[number + 2] = score(jobs[number + 2])
                scores = jnp.where(keeps[part], ahead.pop(number), MASKED)
                held = state[stats, columns]
                old = held[0:1, :]
                new = jnp.maximum(old, jnp.max(scores, axis=0, keepdims=True))
                weights = jnp.exp2(scores * C2 - new * C2)
                factor = jnp.exp2((old - new) * C2)
                total = held[1:2, :] * factor + jnp.sum(weights, axis=0, keepdims=True)
                mixed = lax.dot_general(
                    kv[256:512, lanes],
                    weights.astype(jnp.bfloat16),
                    (((0,), (0,)), ((), ())),
                    preferred_element_type=jnp.float32,
                )
                state[stats, columns] = jnp.concatenate([new, total, held[2:8, :]], axis=0)
                state[lanes, columns] = state[lanes, columns] * factor + mixed

        for kv, number in zip(kvs, blocks, strict=True):
            start = scal[number]
            touches = (start < high_last) & (start + 256 > low_first)

            @pl.when(touches)
            def _(kv=kv, start=start, tile=tile):
                tile(kv, start)


def attend(scal, bounds, q_own, q_par, kvs, blocks, states):
    vmem = pl.BlockSpec(memory_space=pltpu.VMEM)
    first = states is None
    given = () if first else states
    state = jax.ShapeDtypeStruct((544, 256), jnp.float32)
    pairs = 256 * 512 * 4 * len(kvs)
    before = 4 + len(kvs)
    return pl.pallas_call(
        functools.partial(attend_kernel, first, tuple(blocks)),
        out_shape=(state, state),
        in_specs=[pl.BlockSpec(memory_space=pltpu.SMEM)] + [vmem] * (3 + len(kvs) + len(given)),
        out_specs=(vmem, vmem),
        input_output_aliases={} if first else {before: 0, before + 1: 1},
        cost_estimate=pl.CostEstimate(
            flops=4 * pairs * HD, bytes_accessed=1 << 20, transcendentals=pairs
        ),
        compiler_params=pltpu.CompilerParams(vmem_limit_bytes=24 << 20),
        name="attend",
    )(scal, bounds, q_own, q_par, *kvs, *given)


def pack_kernel(top, bottom, out, sems):
    copies = [
        pltpu.make_async_copy(ref, out.at[pl.ds(256 * half, 256)], sems.at[half])
        for half, ref in enumerate((top, bottom))
    ]
    for copy in copies:
        copy.start()
    for copy in copies:
        copy.wait()


def pack(top, bottom):
    return pl.pallas_call(
        pack_kernel,
        out_shape=jax.ShapeDtypeStruct((512, 512), jnp.bfloat16),
        in_specs=[pl.BlockSpec(memory_space=pl.ANY)] * 2,
        out_specs=pl.BlockSpec(memory_space=pltpu.VMEM),
        scratch_shapes=[pltpu.SemaphoreType.DMA((2,))],
        cost_estimate=pl.CostEstimate(flops=0, bytes_accessed=1 << 20, transcendentals=0),
        compiler_params=pltpu.CompilerParams(vmem_limit_bytes=4 << 20),
        name="pack",
    )(top, bottom)


def merge_kernel(mine, other, out):
    for head in range(4):
        at = 512 + 8 * head
        top_a, top_b = mine[at : at + 1, :], other[at : at + 1, :]
        top = jnp.maximum(top_a, top_b)
        f_a, f_b = jnp.exp2((top_a - top) * C2), jnp.exp2((top_b - top) * C2)
        total = mine[at + 1 : at + 2, :] * f_a + other[at + 1 : at + 2, :] * f_b
        rows = slice(head * HD, (head + 1) * HD)
        mixed = (mine[rows, :] * f_a + other[rows, :] * f_b) / total
        out[:, rows] = jnp.transpose(mixed).astype(jnp.bfloat16)


def merge(mine, other):
    vmem = pl.BlockSpec(memory_space=pltpu.VMEM)
    return pl.pallas_call(
        merge_kernel,
        out_shape=jax.ShapeDtypeStruct((256, 512), jnp.bfloat16),
        in_specs=[vmem, vmem],
        out_specs=vmem,
        cost_estimate=pl.CostEstimate(flops=1 << 20, bytes_accessed=1 << 20, transcendentals=4096),
        compiler_params=pltpu.CompilerParams(vmem_limit_bytes=8 << 20),
        name="merge",
    )(mine, other)


def arrange_kernel(scal, *refs):
    out = refs[-1]
    x, y, core, z = scal[24], scal[25], scal[26], scal[27]
    way = 1 - 2 * core
    for number, far in enumerate((0, -1, -2, -3, -4, 1, 2, 3)):
        yy = (y + Y + way * far) % Y
        column = pl.multiple_of((yy % 4) * 128, 128)
        for i in range(X):
            xx = (x + X - i) % X
            slot = (z + Z - (2 * xx + yy // 4)) % Z
            out[slot, pl.ds(column, 128), :] = refs[number][i]


def arrange(scal, groups):
    vmem = pl.BlockSpec(memory_space=pltpu.VMEM)
    return pl.pallas_call(
        arrange_kernel,
        out_shape=jax.ShapeDtypeStruct((Z, 512, 512), jnp.bfloat16),
        in_specs=[pl.BlockSpec(memory_space=pltpu.SMEM)] + [vmem] * len(groups),
        out_specs=vmem,
        cost_estimate=pl.CostEstimate(flops=0, bytes_accessed=8 << 20, transcendentals=0),
        compiler_params=pltpu.CompilerParams(vmem_limit_bytes=16 << 20),
        name="arrange",
    )(scal, *groups)


def project_kernel(slots, partial, *refs):
    count = len(slots)
    weight, out = refs[count], refs[-1]
    total = refs[count + 1][...] if partial else None
    for ref, slot in zip(refs[:count], slots, strict=True):
        term = lax.dot_general(
            ref[...],
            weight[slot],
            (((1,), (1,)), ((), ())),
            preferred_element_type=jnp.float32,
        )
        total = term if total is None else total + term
    out[...] = total.astype(out.dtype)


def project(blocks, slots, weight, partial, last):
    vmem = pl.BlockSpec(memory_space=pltpu.VMEM)
    given = () if partial is None else (partial,)
    return pl.pallas_call(
        functools.partial(project_kernel, tuple(slots), partial is not None),
        out_shape=jax.ShapeDtypeStruct((256, 512), jnp.bfloat16 if last else jnp.float32),
        in_specs=[vmem] * (len(blocks) + 1 + len(given)),
        out_specs=vmem,
        cost_estimate=pl.CostEstimate(
            flops=2 * 256 * 512 * 512 * len(blocks), bytes_accessed=6 << 20, transcendentals=0
        ),
        compiler_params=pltpu.CompilerParams(vmem_limit_bytes=16 << 20),
        name="project",
    )(*blocks, weight, *given)


def local(queries, keys, values, doc_lengths, out_weight):
    s = lax.axis_index("seq").astype(jnp.int32)
    z = lax.axis_index("tp").astype(jnp.int32)
    core, chip = s % 2, s // 2
    rows = queries.shape[0]

    ends = jnp.cumsum(doc_lengths)
    spots = (chip * 2 + jnp.stack([core, 1 - core]))[:, None] * rows + jnp.arange(rows, dtype=jnp.int32)
    ended = ends[:, None, None] <= spots[None]
    low = jnp.max(jnp.where(ended, ends[:, None, None], 0), axis=0)
    high = jnp.min(jnp.where(ended, jnp.int32(1 << 30), ends[:, None, None]), axis=0)
    bounds = jnp.stack([low[0], high[0], low[1], high[1]])
    bounds = jnp.concatenate([bounds, bounds], axis=0)
    way = 1 - 2 * core
    starts = [s * rows]
    for hop in range(1, HOPS + 1):
        there = 2 * (chip - way * hop)
        starts += [(there + core) * rows, (there + 1 - core) * rows]
    starts = jnp.stack(starts + [jnp.int32(0)] * 7)
    edges = jnp.stack([low[:, 0], low[:, -1], high[:, 0], high[:, -1]], axis=1).reshape(8)
    place = jnp.stack([chip // Y, chip % Y, core, z] + [jnp.int32(0)] * 4)
    scal = jnp.concatenate([starts, edges, place])

    mine = pack(keys, values)
    own_chain, par_chain = [mine], [lax.ppermute(mine, "seq", SWAP)]
    q_par = lax.ppermute(queries, "seq", SWAP)
    for _ in range(1, HOPS + 1):
        own_chain.append(lax.ppermute(own_chain[-1], "seq", SIDES))
        par_chain.append(lax.ppermute(par_chain[-1], "seq", SIDES))
    states = None
    for hop in range(HOPS + 1):
        kvs = [mine] if hop == 0 else [own_chain[hop], par_chain[hop]]
        blocks = (0,) if hop == 0 else (2 * hop - 1, 2 * hop)
        states = attend(scal, bounds, queries, q_par, kvs, blocks, states)

    piece = lax.ppermute(out_weight.T, ("seq", "tp"), TURN)
    beside = lax.ppermute(piece, "seq", SWAP)
    piece = jnp.where(
        core == 0,
        jnp.concatenate([piece, beside], axis=0),
        jnp.concatenate([beside, piece], axis=0),
    )
    line = [piece]
    for far in range(1, X):
        line.append(lax.ppermute(piece, "seq", X_FAR[far]))
    groups = [jnp.stack(line)]
    for _ in range(1, 5):
        groups.append(lax.ppermute(groups[-1], "seq", Y_WAYS))
    groups += [lax.ppermute(groups[far], "seq", SWAP) for far in range(1, 4)]
    weight = arrange(scal, groups)

    other = lax.ppermute(states[1], "seq", SWAP)
    attended = merge(states[0], other)
    up, down = [attended], [attended]
    for far in range(1, 5):
        up.append(lax.ppermute(up[-1], "tp", Z_UP))
        if far < 4:
            down.append(lax.ppermute(down[-1], "tp", Z_DOWN))
    partial = project(up[:4] + down[1:3], (0, 1, 2, 3, 7, 6), weight, None, False)
    return project([up[4], down[3]], (4, 5), weight, partial, True)


def solution(mesh):
    in_specs = (P("seq", "tp"), P("seq", "tp"), P("seq", "tp"), P(), P("tp", "seq"))
    return jax.shard_map(
        local, mesh=mesh, in_specs=in_specs, out_specs=P("seq", "tp"), check_vma=False
    )
```

```python
import functools
import math

import jax
import jax.numpy as jnp
from jax import lax
from jax.experimental import pallas as pl
from jax.experimental.pallas import tpu as pltpu
from jax.sharding import PartitionSpec as P


HD = 128
X, Y, Z = 4, 8, 8
HOPS = 4
LOW = -1e30
MASKED = -3e37
C2 = math.log2(math.e) / math.sqrt(HD)


def device(x, y, core):
    return ((x % X) * Y + y % Y) * 2 + core


def pairs_of(step):
    return [
        (device(x, y, core), device(*step(x, y, core)))
        for x in range(X)
        for y in range(Y)
        for core in range(2)
    ]


SWAP = pairs_of(lambda x, y, core: (x, y, 1 - core))
SIDES = [(s, s + 2 - 4 * (s % 2)) for s in range(2 * X * Y) if 0 <= s + 2 - 4 * (s % 2) < 2 * X * Y]
Z_UP = [(z, (z + 1) % Z) for z in range(Z)]
Z_DOWN = [(z, (z - 1) % Z) for z in range(Z)]
TURN = [
    ((8 * a + j) * Z + b, (8 * b + j) * Z + a) for a in range(Z) for b in range(Z) for j in range(8)
]


def attend_kernel(first, blocks, scal, bounds, q_own, q_par, *refs):
    count = len(blocks)
    kvs = refs[:count]
    if first:
        outs = refs[count:]
        for out in outs:
            out[0:512, :] = jnp.zeros((512, 256), jnp.float32)
            row = lax.broadcasted_iota(jnp.int32, (32, 256), 0)
            out[512:544, :] = jnp.where(row % 8 == 0, LOW, 0.0)
    else:
        ins = refs[count : count + 2]
        outs = refs[count + 2 :]
        for given, out in zip(ins, outs, strict=True):
            out[...] = given[...]

    for half, (q_ref, state) in enumerate(zip((q_own, q_par), outs, strict=True)):
        low_first, high_last = scal[16 + 4 * half], scal[19 + 4 * half]

        def tile(kv, start, half=half, q_ref=q_ref, state=state):
            wide = 256
            spot = lax.broadcasted_iota(jnp.int32, (256, wide), 0) + start
            jobs = [(head, part) for part in range(256 // wide) for head in range(4)]

            def score(job):
                head, part = job
                lanes = slice(head * HD, (head + 1) * HD)
                return lax.dot_general(
                    kv[0:256, lanes],
                    q_ref[part * wide : (part + 1) * wide, lanes],
                    (((1,), (1,)), ((), ())),
                    preferred_element_type=jnp.float32,
                )

            keeps = []
            for part in range(256 // wide):
                columns = slice(part * wide, (part + 1) * wide)
                keeps.append(
                    (spot >= bounds[2 * half : 2 * half + 1, columns])
                    & (spot < bounds[2 * half + 1 : 2 * half + 2, columns])
                )
            ahead = {number: score(jobs[number]) for number in range(2)}
            for number, (head, part) in enumerate(jobs):
                columns = slice(part * wide, (part + 1) * wide)
                lanes = slice(head * HD, (head + 1) * HD)
                stats = slice(512 + 8 * head, 520 + 8 * head)
                if number + 2 < len(jobs):
                    ahead[number + 2] = score(jobs[number + 2])
                scores = jnp.where(keeps[part], ahead.pop(number), MASKED)
                held = state[stats, columns]
                old = held[0:1, :]
                new = jnp.maximum(old, jnp.max(scores, axis=0, keepdims=True))
                weights = jnp.exp2(scores * C2 - new * C2)
                factor = jnp.exp2((old - new) * C2)
                total = held[1:2, :] * factor + jnp.sum(weights, axis=0, keepdims=True)
                mixed = lax.dot_general(
                    kv[256:512, lanes],
                    weights.astype(jnp.bfloat16),
                    (((0,), (0,)), ((), ())),
                    preferred_element_type=jnp.float32,
                )
                state[stats, columns] = jnp.concatenate([new, total, held[2:8, :]], axis=0)
                state[lanes, columns] = state[lanes, columns] * factor + mixed

        for kv, number in zip(kvs, blocks, strict=True):
            start = scal[number]
            touches = (start < high_last) & (start + 256 > low_first)

            @pl.when(touches)
            def _(kv=kv, start=start, tile=tile):
                tile(kv, start)


def attend(scal, bounds, q_own, q_par, kvs, blocks, states):
    vmem = pl.BlockSpec(memory_space=pltpu.VMEM)
    first = states is None
    given = () if first else states
    state = jax.ShapeDtypeStruct((544, 256), jnp.float32)
    pairs = 256 * 512 * 4 * len(kvs)
    before = 4 + len(kvs)
    return pl.pallas_call(
        functools.partial(attend_kernel, first, tuple(blocks)),
        out_shape=(state, state),
        in_specs=[pl.BlockSpec(memory_space=pltpu.SMEM)] + [vmem] * (3 + len(kvs) + len(given)),
        out_specs=(vmem, vmem),
        input_output_aliases={} if first else {before: 0, before + 1: 1},
        cost_estimate=pl.CostEstimate(
            flops=4 * pairs * HD, bytes_accessed=1 << 20, transcendentals=pairs
        ),
        compiler_params=pltpu.CompilerParams(vmem_limit_bytes=24 << 20),
        name="attend",
    )(scal, bounds, q_own, q_par, *kvs, *given)


def pack_kernel(top, bottom, out, sems):
    copies = [
        pltpu.make_async_copy(ref, out.at[pl.ds(256 * half, 256)], sems.at[half])
        for half, ref in enumerate((top, bottom))
    ]
    for copy in copies:
        copy.start()
    for copy in copies:
        copy.wait()


def pack(top, bottom):
    return pl.pallas_call(
        pack_kernel,
        out_shape=jax.ShapeDtypeStruct((512, 512), jnp.bfloat16),
        in_specs=[pl.BlockSpec(memory_space=pl.ANY)] * 2,
        out_specs=pl.BlockSpec(memory_space=pltpu.VMEM),
        scratch_shapes=[pltpu.SemaphoreType.DMA((2,))],
        cost_estimate=pl.CostEstimate(flops=0, bytes_accessed=1 << 20, transcendentals=0),
        compiler_params=pltpu.CompilerParams(vmem_limit_bytes=4 << 20),
        name="pack",
    )(top, bottom)


def hold_kernel(given, out):
    out[...] = given[...]


def hold(value):
    vmem = pl.BlockSpec(memory_space=pltpu.VMEM)
    return pl.pallas_call(
        hold_kernel,
        out_shape=jax.ShapeDtypeStruct(value.shape, value.dtype),
        in_specs=[vmem],
        out_specs=vmem,
        cost_estimate=pl.CostEstimate(flops=0, bytes_accessed=1 << 17, transcendentals=0),
        compiler_params=pltpu.CompilerParams(vmem_limit_bytes=4 << 20),
        name="hold",
    )(value)


def merge_kernel(mine, other, out):
    for head in range(4):
        at = 512 + 8 * head
        top_a, top_b = mine[at : at + 1, :], other[at : at + 1, :]
        top = jnp.maximum(top_a, top_b)
        f_a, f_b = jnp.exp2((top_a - top) * C2), jnp.exp2((top_b - top) * C2)
        total = mine[at + 1 : at + 2, :] * f_a + other[at + 1 : at + 2, :] * f_b
        rows = slice(head * HD, (head + 1) * HD)
        mixed = (mine[rows, :] * f_a + other[rows, :] * f_b) / total
        out[:, rows] = jnp.transpose(mixed).astype(jnp.bfloat16)


def merge(mine, other):
    vmem = pl.BlockSpec(memory_space=pltpu.VMEM)
    return pl.pallas_call(
        merge_kernel,
        out_shape=jax.ShapeDtypeStruct((256, 512), jnp.bfloat16),
        in_specs=[vmem, vmem],
        out_specs=vmem,
        cost_estimate=pl.CostEstimate(flops=1 << 20, bytes_accessed=1 << 20, transcendentals=4096),
        compiler_params=pltpu.CompilerParams(vmem_limit_bytes=8 << 20),
        name="merge",
    )(mine, other)


def project_kernel(slots, partial, scal, *refs):
    count = len(slots)
    weight, out = refs[count], refs[-1]
    total = refs[count + 1][...] if partial else None
    for ref, slot in zip(refs[:count], slots, strict=True):
        term = lax.dot_general(
            ref[...],
            weight[(scal[27] + slot) % Z],
            (((1,), (1,)), ((), ())),
            preferred_element_type=jnp.float32,
        )
        total = term if total is None else total + term
    out[...] = total.astype(out.dtype)


def project(scal, blocks, slots, weight, partial, last):
    vmem = pl.BlockSpec(memory_space=pltpu.VMEM)
    given = () if partial is None else (partial,)
    return pl.pallas_call(
        functools.partial(project_kernel, tuple(slots), partial is not None),
        out_shape=jax.ShapeDtypeStruct((256, 512), jnp.bfloat16 if last else jnp.float32),
        in_specs=[pl.BlockSpec(memory_space=pltpu.SMEM)] + [vmem] * (len(blocks) + 1 + len(given)),
        out_specs=vmem,
        cost_estimate=pl.CostEstimate(
            flops=2 * 256 * 512 * 512 * len(blocks), bytes_accessed=6 << 20, transcendentals=0
        ),
        compiler_params=pltpu.CompilerParams(vmem_limit_bytes=16 << 20),
        name="project",
    )(scal, *blocks, weight, *given)


def local(queries, keys, values, doc_lengths, out_weight):
    s = lax.axis_index("seq").astype(jnp.int32)
    z = lax.axis_index("tp").astype(jnp.int32)
    core, chip = s % 2, s // 2
    rows = queries.shape[0]

    ends = jnp.cumsum(doc_lengths)
    spots = (chip * 2 + jnp.stack([core, 1 - core]))[:, None] * rows + jnp.arange(rows, dtype=jnp.int32)
    ended = ends[:, None, None] <= spots[None]
    low = jnp.max(jnp.where(ended, ends[:, None, None], 0), axis=0)
    high = jnp.min(jnp.where(ended, jnp.int32(1 << 30), ends[:, None, None]), axis=0)
    bounds = jnp.stack([low[0], high[0], low[1], high[1]])
    bounds = jnp.concatenate([bounds, bounds], axis=0)
    way = 1 - 2 * core
    starts = [s * rows]
    for hop in range(1, HOPS + 1):
        there = 2 * (chip - way * hop)
        starts += [(there + core) * rows, (there + 1 - core) * rows]
    starts = jnp.stack(starts + [jnp.int32(0)] * 7)
    edges = jnp.stack([low[:, 0], low[:, -1], high[:, 0], high[:, -1]], axis=1).reshape(8)
    place = jnp.stack([chip // Y, chip % Y, core, z] + [jnp.int32(0)] * 4)
    scal = jnp.concatenate([starts, edges, place])

    mine = pack(keys, values)
    own_chain, par_chain = [mine], [lax.ppermute(mine, "seq", SWAP)]
    q_par = lax.ppermute(queries, "seq", SWAP)
    for _ in range(1, HOPS + 1):
        own_chain.append(lax.ppermute(own_chain[-1], "seq", SIDES))
        par_chain.append(lax.ppermute(par_chain[-1], "seq", SIDES))
    states = None
    for hop in range(HOPS + 1):
        kvs = [mine] if hop == 0 else [own_chain[hop], par_chain[hop]]
        blocks = (0,) if hop == 0 else (2 * hop - 1, 2 * hop)
        states = attend(scal, bounds, queries, q_par, kvs, blocks, states)

    piece = lax.ppermute(out_weight.T, ("seq", "tp"), TURN)
    piece = hold(piece)
    weight = lax.all_gather(piece, "seq", axis=0, tiled=True).reshape(Z, 512, 512)

    other = lax.ppermute(states[1], "seq", SWAP)
    attended = merge(states[0], other)
    up, down = [attended], [attended]
    for far in range(1, 5):
        up.append(lax.ppermute(up[-1], "tp", Z_UP))
        if far < 4:
            down.append(lax.ppermute(down[-1], "tp", Z_DOWN))
    partial = project(scal, up[:4] + down[1:3], (8, 7, 6, 5, 1, 2), weight, None, False)
    return project(scal, [up[4], down[3]], (4, 3), weight, partial, True)


def solution(mesh):
    in_specs = (P("seq", "tp"), P("seq", "tp"), P("seq", "tp"), P(), P("tp", "seq"))
    return jax.shard_map(
        local, mesh=mesh, in_specs=in_specs, out_specs=P("seq", "tp"), check_vma=False
    )
```
